128 devices in a mesh: ha: 8 (over z, x_hi), wa: 16 (over x_lo, y, core).
Axes of the slice: x: 4 (x_hi: 2, x_lo: 2; x = x_hi * 2 + x_lo), y: 4, z: 4, core: 2. Of those that a mesh axis runs over, the one named last changes fastest.
Arguments:
- queries: bfloat16 [8, 16, 384, 1536], P('ha', 'wa'), may hold values from -15 to 15
- keys_values: bfloat16 [8, 16, 3, 2, 384, 1536], P('ha', 'wa'), may hold values from -9 to 9
- far_offsets: int32 [16, 8, 12, 2], P('wa', 'ha'), may hold values from 0 to 14, all different within a row; in each aligned block of 12 rows (0 to 11, 12 to 23, ..., all dimensions but the last counted through in order) at most 2 rows name the same one
Outputs:
- attended: bfloat16 [8, 16, 384, 1536], P('ha', 'wa')
The draws below stay inside these ranges and needn't reach their ends.
Inputs may be any that keep to these rules, and one draw needn't show every extreme that they name: `far_offsets`: within the rows of one device (one tile column w, its 1 tile rows, all heads) each offset is named by at most 2 of those rows; each row names 2 different offsets.
All inputs are finite; a program needn't handle non-finite values.
Results may differ from the reference program's by a relative error of at most 0.0048.
Values may be sent and summed in bfloat16 or wider, within the bound.
A program may use at most 320 MiB of HBM per device.

```python
import math
import jax
import jax.numpy as jnp
import numpy as np
from jax import lax

HEADS = 12
HD = 128
TILE = 384
TT = 3
FAR = 2
TH_DEV = 1
GH = 8
GW = 16
SPAN = 15
CAP = 2


def draw_queries(key, part):
    shape = (GH, GW, TILE, HEADS * HD)
    base = jnp.clip(jax.random.normal(jax.random.fold_in(key, 1), shape, jnp.float32), -6.0, 6.0)
    return base.astype(jnp.bfloat16)


def draw_keys_values(key, part):
    shape = (GH, GW, TT, 2, TILE, HEADS * HD)
    base = jnp.clip(jax.random.normal(jax.random.fold_in(key, 2), shape, jnp.float32), -6.0, 6.0)
    return base.astype(jnp.bfloat16)


def assign_block(stream_key, own, number, rows, count, top, bound, lean):
    ranking = jax.random.permutation(stream_key, count)
    heavy_load, common = portions_of(count, rows * top, bound, lean, True), portions_of(count, rows * top, bound, lean, False)
    places = jnp.arange(count)

    def named(lengths, turn):
        used = int((lengths > 0).sum())
        fixed = max(1, used // 4)
        passed = fixed + (places - fixed + turn * (used - fixed)) % max(1, count - fixed)
        return jnp.zeros((count,), jnp.int32).at[ranking[jnp.where(places < fixed, places, passed)]].set(jnp.asarray(lengths, jnp.int32))

    lengths = jnp.where(number % 4 == 0, named(heavy_load, number // 4), named(common, number - number // 4 - 1))
    mixed = jax.random.permutation(jax.random.fold_in(own, 3), count)
    source_of, sink = mixed[0:count // 2 * 2:2], mixed[1:count // 2 * 2:2]
    room = jnp.minimum(lengths[source_of] - 1, bound - lengths[sink]) // 2
    room = jnp.where((source_of == ranking[0]) | (sink == ranking[0]) | (lengths[sink] == 0), 0, jnp.maximum(room, 0))
    passed = jax.random.randint(jax.random.fold_in(own, 4), (count // 2,), 0, 1 << 20) % (room + 1)
    lengths = lengths.at[source_of].add(-passed).at[sink].add(passed)
    members = jnp.searchsorted(jnp.cumsum(lengths), jnp.arange(rows * top), side="right").astype(jnp.int32)
    table = members.reshape(top, rows).T
    table = table[jax.random.permutation(jax.random.fold_in(own, 1), rows)]
    turn = jax.random.randint(jax.random.fold_in(own, 2), (rows, 1), 0, top)
    return jnp.take_along_axis(table, (jnp.arange(top)[None, :] + turn) % top, axis=1)


def portions_of(number_of, total, reach, skew, full):
    portions = [(1 << 20) // math.isqrt(standing ** skew) + 1 for standing in range(1, number_of + 1)]
    largest = reach if full else min(reach, max(-(-total // number_of), total * portions[0] // sum(portions)))
    least = 1 if total - largest >= number_of - 1 else 0
    holding, spare = [largest] + [least] * (number_of - 1), total - largest - least * (number_of - 1)
    while spare > 0:
        candidates = [i for i in range(1, number_of) if holding[i] < largest] or [i for i in range(1, number_of) if holding[i] < reach]
        pool, remaining = sum([portions[i] for i in candidates]), spare
        for i in candidates:
            addition = min(reach - holding[i], max(1, remaining * portions[i] // pool), spare)
            holding[i] = holding[i] + addition
            spare = spare - addition
    return np.array(holding)


def setup_inputs(seed: int = 0) -> dict:
    key_of = jax.random.split(jax.random.key(seed), 4)
    queries = draw_queries(jax.random.fold_in(key_of[3], 71), 0)
    keys_values = draw_keys_values(jax.random.fold_in(key_of[3], 71), 0)
    far_offsets_keys = jax.random.split(jax.random.fold_in(key_of[2], 1), GW * GH * HEADS // (TH_DEV * HEADS))
    far_offsets_turns = jax.random.permutation(jax.random.fold_in(key_of[2], 3), GW * GH * HEADS // (TH_DEV * HEADS))
    far_offsets = jax.vmap(lambda own, number: assign_block(jax.random.fold_in(key_of[2], 2), own, number, TH_DEV * HEADS, SPAN, FAR, CAP, 2))(far_offsets_keys, far_offsets_turns).reshape((GW, GH, HEADS, FAR))
    return {"queries": queries, "keys_values": keys_values, "far_offsets": far_offsets}


def attend(head_queries, key_tiles, value_tiles, key_mask):
    score_scale = 1.0 / (HD ** 0.5)
    scores = jnp.einsum("iqd,ikd->iqk", head_queries.astype(jnp.float32), key_tiles.astype(jnp.float32)) * score_scale
    scores = jnp.where(key_mask, scores, -1e30)
    peak_score = jnp.max(scores, axis=2, keepdims=True)
    weights = jnp.exp(scores - peak_score)
    totals = jnp.sum(weights, axis=2, keepdims=True)
    rounded = lax.optimization_barrier(weights.astype(jnp.bfloat16)).astype(jnp.float32)
    summed = jnp.einsum("iqk,ikd->iqd", rounded, value_tiles.astype(jnp.float32))
    return (summed / totals).astype(jnp.bfloat16)


def reference(queries, keys_values, far_offsets):
    padded = jnp.pad(keys_values, ((1, 1), (1, 1), (0, 0), (0, 0), (0, 0), (0, 0)))
    columns = jnp.arange(GW, dtype=jnp.int32)
    steps_three = jnp.arange(3, dtype=jnp.int32)

    def one_row(tile_row):
        row_slab = lax.dynamic_slice_in_dim(padded, tile_row, 3, 0)
        row_tiles = lax.dynamic_index_in_dim(keys_values, tile_row, 0, keepdims=False)
        row_queries = lax.dynamic_index_in_dim(queries, tile_row, 0, keepdims=False)
        offset_rows = lax.dynamic_index_in_dim(far_offsets, tile_row, 1, keepdims=False)
        row_inside = (tile_row + steps_three - 1 >= 0) & (tile_row + steps_three - 1 < GH)
        col_inside = (columns[:, None] + steps_three[None, :] - 1 >= 0) & (columns[:, None] + steps_three[None, :] - 1 < GW)
        inside = row_inside[None, :, None] & col_inside[:, None, :]
        key_mask = jnp.concatenate([jnp.repeat(inside.reshape(GW, 9), TT * TILE, axis=1), jnp.ones((GW, FAR * TILE), dtype=bool)], axis=1)[:, None, :]

        def one_head(head_index):
            head_queries = lax.dynamic_slice_in_dim(row_queries, head_index * HD, HD, 2)
            head_slab = lax.dynamic_slice_in_dim(row_slab, head_index * HD, HD, 5)
            window = jnp.stack([head_slab[:, col_step:col_step + GW] for col_step in range(3)], axis=2)
            window = jnp.transpose(window, (1, 0, 2, 3, 4, 5, 6))
            head_offsets = jnp.take(offset_rows, head_index, axis=1)
            source = ((columns[:, None] + 1 + head_offsets) % GW).astype(jnp.int32)
            head_tiles = lax.dynamic_slice_in_dim(row_tiles, head_index * HD, HD, 4)[:, 1]
            far_tiles = head_tiles[source]
            key_tiles = jnp.concatenate([window[:, :, :, :, 0].reshape(GW, 9 * TT * TILE, HD), far_tiles[:, :, 0].reshape(GW, FAR * TILE, HD)], axis=1)
            value_tiles = jnp.concatenate([window[:, :, :, :, 1].reshape(GW, 9 * TT * TILE, HD), far_tiles[:, :, 1].reshape(GW, FAR * TILE, HD)], axis=1)
            return attend(head_queries, key_tiles, value_tiles, key_mask)

        per_head = lax.map(one_head, jnp.arange(HEADS, dtype=jnp.int32))
        return jnp.transpose(per_head, (1, 2, 0, 3)).reshape(GW, TILE, HEADS * HD)

    return lax.map(one_row, jnp.arange(GH, dtype=jnp.int32))
```

```python
import jax
import jax.numpy as jnp
from jax import lax
from jax.experimental import pallas as pl
from jax.experimental.pallas import tpu as pltpu
from jax.sharding import PartitionSpec as P

HEADS = 12
HD = 128
TILE = 384
TT = 3
FAR = 2
CAP = 2
NC = 3
HC = HEADS // NC
CW = HC * HD
TO_LOG2 = 1.4426950408889634 / HD**0.5
MESH = pl.DeviceIdType.MESH


def pack_far(off_ref, q_ref, slot_ref, qf_ref, qt_ref, heads, count):
    spans = qf_ref.shape[0] // CAP

    def clear(i, carry):
        heads[i] = 0
        count[i] = 0
        return carry

    lax.fori_loop(0, spans * CAP, clear, 0)
    qf_ref[...] = jnp.zeros_like(qf_ref)

    def place(i, carry):
        offset = off_ref[i]
        taken = count[offset]
        count[offset] = taken + 1
        slot = offset * CAP + jnp.minimum(taken, CAP - 1)
        head = i // FAR
        slot_ref[i] = slot
        heads[slot] = head
        qf_ref[slot] = q_ref[:, pl.ds(pl.multiple_of(head * HD, HD), HD)]
        return carry

    lax.fori_loop(0, HEADS * FAR, place, 0)
    lane = lax.broadcasted_iota(jnp.int32, (8, HD), 1)
    for s in range(spans):
        qt_ref[s] = jnp.where(lane == 0, heads[s * CAP], heads[s * CAP + 1])


def attend(q, k, v_one):
    s = lax.dot_general(q, k, (((1,), (1,)), ((), ())), preferred_element_type=jnp.float32)
    peak = jnp.max(s, axis=1, keepdims=True)
    p = jnp.exp2(s * TO_LOG2 - peak * TO_LOG2)
    both = jnp.dot(p.astype(jnp.bfloat16), v_one, preferred_element_type=jnp.float32)
    total = both[:, HD:]
    return (both[:, :HD] * (1.0 / total)).astype(jnp.bfloat16), peak * TO_LOG2 + jnp.log2(total)


def with_ones(v):
    return jnp.concatenate([v, jnp.ones(v.shape, v.dtype)], axis=1)


def blend_weights(rows):
    peak = rows[0]
    for row in rows[1:]:
        peak = jnp.maximum(peak, row)
    parts = [jnp.exp2(row - peak) for row in rows]
    total = parts[0]
    for part in parts[1:]:
        total = total + part
    inverse = 1.0 / total
    stack = [part * inverse for part in parts]
    stack.append(jnp.zeros((HD - 8 * len(rows), TILE), jnp.float32))
    return jnp.transpose(jnp.concatenate(stack, axis=0)), peak + jnp.log2(total)


def fused(
    spans, rows_ha, cols_wa, slot_ref, q_ref, kv_ref, qf_ref, qt_ref, out_ref,
    QW, KV, O, LO, OI, LI, ZS, ZL, ZI, ZLI, XS, XL, XI, XLI, FQ, TI, TS, FO, FL, FI, FLI, FLX, AC,
    kv_sem, q_sem, t_sem, v_s, v_r, z_s, z_r, h_s, h_r, o_s, o_r, l_s, l_r,
    zo_s, zo_r, zl_s, zl_r, xo_s, xo_r, xl_s, xl_r, fq_s, fq_r, ft_s, ft_r, fo_s, fo_r, fl_s, fl_r,
):
    h = lax.axis_index("ha")
    w = lax.axis_index("wa")
    sign = 1 - 2 * (h % 2)
    partner = h + sign
    z_to = (h + 2 * sign + rows_ha) % rows_ha
    z_from = (h - 2 * sign + rows_ha) % rows_ha
    left = (w + cols_wa - 1) % cols_wa
    right = (w + 1) % cols_wa
    has_left = w > 0
    has_right = w < cols_wa - 1
    has_far_row = (h + 2 * sign >= 0) & (h + 2 * sign < rows_ha)

    def cols_of(c):
        return pl.ds(pl.multiple_of(c * CW, CW), CW)

    def remote(src, dst, ss, rs, ha=None, wa=None):
        return pltpu.make_async_remote_copy(
            src_ref=src, dst_ref=dst, send_sem=ss, recv_sem=rs,
            device_id={"ha": h if ha is None else ha, "wa": w if wa is None else wa},
            device_id_type=MESH,
        )

    def kv_in(c):
        cols = pl.ds(pl.multiple_of(c * HD, HD), HD)
        return pltpu.make_async_copy(kv_ref.at[:, :, :, cols], KV.at[c], kv_sem.at[c])

    def q_in(c):
        return pltpu.make_async_copy(q_ref.at[:, cols_of(c)], QW.at[0, c], q_sem.at[c])

    def send_v(c):
        return remote(q_ref.at[:, cols_of(c)], QW.at[3, c], v_s.at[c], v_r.at[c], ha=partner)

    def send_z(c):
        return remote(QW.at[3, c], QW.at[6, c], z_s.at[c], z_r.at[c], ha=z_to)

    def send_h(r, side, c):
        src = q_ref.at[:, cols_of(c)] if r == 0 else QW.at[3 * r, c]
        i = r * 2 + side
        return remote(
            src, QW.at[3 * r + 2 - side, c], h_s.at[i, c], h_r.at[i, c],
            wa=right if side else left,
        )

    def send_o(r, side, c):
        i = r * 2 + side
        return (
            remote(O.at[3 * r + 1 + side, c], OI.at[r * 2 + 1 - side, c], o_s.at[i, c], o_r.at[i, c],
                   wa=right if side else left),
            remote(LO.at[3 * r + 1 + side, c], LI.at[r * 2 + 1 - side, c], l_s.at[i, c], l_r.at[i, c],
                   wa=right if side else left),
        )

    def send_zo(c):
        return (
            remote(ZS.at[c], ZI.at[c], zo_s.at[c], zo_r.at[c], ha=z_from),
            remote(ZL.at[c], ZLI.at[c], zl_s.at[c], zl_r.at[c], ha=z_from),
        )

    def send_xo(c):
        return (
            remote(XS.at[c], XI.at[c], xo_s.at[c], xo_r.at[c], ha=partner),
            remote(XL.at[c], XLI.at[c], xl_s.at[c], xl_r.at[c], ha=partner),
        )

    def send_fq(s):
        owner = (w + 1 + s) % cols_wa
        return (
            remote(qt_ref.at[s], TI.at[s], ft_s.at[s], ft_r.at[s], wa=owner),
            remote(qf_ref.at[pl.ds(s * CAP, CAP)], FQ.at[pl.ds(s * CAP, CAP)], fq_s.at[s], fq_r.at[s], wa=owner),
        )

    def send_fo(s):
        asker = (w + 2 * cols_wa - 1 - s) % cols_wa
        return (
            remote(FO.at[pl.ds(s * CAP, CAP)], FI.at[pl.ds(s * CAP, CAP)], fo_s.at[s], fo_r.at[s], wa=asker),
            remote(FL.at[s], FLI.at[s], fl_s.at[s], fl_r.at[s], wa=asker),
        )

    def chunks(step):
        def run(c, carry):
            step(c)
            return carry

        lax.fori_loop(0, NC, run, 0)

    def kv_start(head, carry):
        kv_in(head).start()
        return carry

    lax.fori_loop(0, HEADS, kv_start, 0)

    @chunks
    def _(c):
        q_in(c).start()
        send_v(c).start()

    @chunks
    def _(c):
        send_h(0, 0, c).start()
        send_h(0, 1, c).start()

    def far_out(s, carry):
        for copy in send_fq(s):
            copy.start()
        return carry

    lax.fori_loop(0, spans, far_out, 0)

    AC[...] = jnp.zeros_like(AC)
    lane = lax.broadcasted_iota(jnp.int32, (TILE, HD), 1)

    def head_cols(hh):
        return pl.ds(pl.multiple_of(hh * HD, HD), HD)

    def keys_values_of(head):
        k = KV[head, :, 0].reshape(TT * TILE, HD)
        v = KV[head, :, 1].reshape(TT * TILE, HD)
        return k, with_ones(v)

    def pair(a, b, c):
        def step(hh, carry):
            cols = head_cols(hh)
            k, v = keys_values_of(c * HC + hh)
            for i, slot in enumerate((a, b)):
                o, l = attend(QW[slot, c, :, cols], k, v)
                O[slot, c, :, cols] = o
                AC[i] = jnp.where(lane == hh, l, AC[i])
            return carry

        lax.fori_loop(0, HC, step, 0)
        for i, slot in enumerate((a, b)):
            LO[slot, c] = jnp.transpose(AC[i])[:8]

    @chunks
    def _(c):
        for hh in range(HC):
            kv_in(c * HC + hh).wait()
        q_in(c).wait()

        def step(half, carry):
            for e in range(2):
                hh = half * 2 + e
                cols = head_cols(hh)
                k, v = keys_values_of(c * HC + hh)
                o, l = attend(QW[0, c, :, cols], k, v)
                O[0, c, :, cols] = o
                AC[0] = jnp.where(lane == hh, l, AC[0])
            return carry

        lax.fori_loop(0, HC // 2, step, 0)
        LO[0, c] = jnp.transpose(AC[0])[:8]

    def give_back(r, c):
        for side in range(2):
            for copy in send_o(r, side, c):
                copy.start()

    @chunks
    def _(c):
        send_h(0, 0, c).wait_recv()
        send_h(0, 1, c).wait_recv()
        pair(1, 2, c)
        give_back(0, c)
        send_v(c).wait_recv()
        send_z(c).start()
        send_h(1, 0, c).start()
        send_h(1, 1, c).start()

    @chunks
    def _(c):
        send_z(c).wait_recv()
        send_h(2, 0, c).start()
        send_h(2, 1, c).start()
        pair(3, 6, c)

    def far_step(s, carry):
        for copy in send_fq(s):
            copy.wait_recv()
        table = pltpu.make_async_copy(TI.at[s], TS, t_sem)
        table.start()
        table.wait()
        for p in range(CAP):
            head = TS[0, p]
            o, l = attend(FQ[s * CAP + p], KV[head, 1, 0], with_ones(KV[head, 1, 1]))
            FO[s * CAP + p] = o
            AC[0] = jnp.where(lane == p, l, AC[0])
        FL[s] = jnp.transpose(AC[0])[:8]
        for copy in send_fo(s):
            copy.start()
        return carry

    lax.fori_loop(0, spans, far_step, 0)

    for r in (2, 1):

        @chunks
        def _(c):
            send_h(r, 0, c).wait_recv()
            send_h(r, 1, c).wait_recv()
            pair(3 * r + 1, 3 * r + 2, c)
            give_back(r, c)

    def arrived(r, c):
        for side in range(2):
            for copy in send_o(r, side, c):
                copy.wait_recv()

    def masked(row, ok):
        return jnp.where(ok, row, -1e30)

    def row_parts(r, c):
        outs = [O.at[3 * r, c], OI.at[2 * r, c], OI.at[2 * r + 1, c]]
        rows = [LO[3 * r, c], masked(LI[2 * r, c], has_left), masked(LI[2 * r + 1, c], has_right)]
        return outs, rows

    def blend(outs, weights, hh):
        total = None
        for i, o in enumerate(outs):
            term = o.astype(jnp.float32) * weights[:, i * 8 + hh : i * 8 + hh + 1]
            total = term if total is None else total + term
        return total.astype(jnp.bfloat16)

    @chunks
    def _(c):
        arrived(2, c)
        outs, rows = row_parts(2, c)
        weights, joint = blend_weights(rows)
        ZL[c] = joint
        for hh in range(HC):
            cols = slice(hh * HD, (hh + 1) * HD)
            ZS[c, :, cols] = blend([o[:, cols] for o in outs], weights, hh)
        for copy in send_zo(c):
            copy.start()

    @chunks
    def _(c):
        arrived(1, c)
        for copy in send_zo(c):
            copy.wait_recv()
        outs, rows = row_parts(1, c)
        outs.append(ZI.at[c])
        rows.append(masked(ZLI[c], has_far_row))
        weights, joint = blend_weights(rows)
        XL[c] = joint
        for hh in range(HC):
            cols = slice(hh * HD, (hh + 1) * HD)
            XS[c, :, cols] = blend([o[:, cols] for o in outs], weights, hh)
        for copy in send_xo(c):
            copy.start()

    def far_in(s, carry):
        for copy in send_fo(s):
            copy.wait_recv()
        for p in range(CAP):
            FLX[s * CAP + p] = FLI[s, p : p + 1, :]
        return carry

    lax.fori_loop(0, spans, far_in, 0)

    @chunks
    def _(c):
        arrived(0, c)
        for copy in send_xo(c):
            copy.wait_recv()
        outs, rows = row_parts(0, c)
        outs.append(XI.at[c])
        rows.append(XLI[c])
        far = [[slot_ref[(c * HC + hh) * FAR + f] for hh in range(HC)] for f in range(FAR)]
        for f in range(FAR):
            lines = [FLX[slot] for slot in far[f]]
            lines.append(jnp.zeros((8 - HC, TILE), jnp.float32))
            rows.append(jnp.concatenate(lines, axis=0))
        weights, _joint = blend_weights(rows)
        for hh in range(HC):
            cols = slice(hh * HD, (hh + 1) * HD)
            values = [o[:, cols] for o in outs] + [FI[far[f][hh]] for f in range(FAR)]
            out_ref[:, pl.ds(pl.multiple_of(c * CW + hh * HD, HD), HD)] = blend(values, weights, hh)

    @chunks
    def _(c):
        send_v(c).wait_send()
        send_z(c).wait_send()
        for r in range(3):
            for side in range(2):
                send_h(r, side, c).wait_send()
                for copy in send_o(r, side, c):
                    copy.wait_send()
        for copy in send_zo(c) + send_xo(c):
            copy.wait_send()

    def far_done(s, carry):
        for copy in send_fq(s) + send_fo(s):
            copy.wait_send()
        return carry

    lax.fori_loop(0, spans, far_done, 0)


def solution(mesh):
    rows_ha, cols_wa = mesh.shape["ha"], mesh.shape["wa"]
    spans = cols_wa - 1
    bf16, f32 = jnp.bfloat16, jnp.float32
    any_space = pl.BlockSpec(memory_space=pl.ANY)
    smem = pl.BlockSpec(memory_space=pltpu.SMEM)
    vmem = pl.BlockSpec(memory_space=pltpu.VMEM)

    def tiles(*lead):
        return pltpu.VMEM((*lead, TILE, CW), bf16)

    def lines(*lead):
        return pltpu.VMEM((*lead, 8, TILE), f32)

    def sems(*dims):
        return [pltpu.SemaphoreType.DMA(dims)] * 2

    def on_device(queries, keys_values, far_offsets):
        q = queries[0, 0]
        slots, qf, qt = pl.pallas_call(
            pack_far,
            out_shape=(
                jax.ShapeDtypeStruct((HEADS * FAR,), jnp.int32),
                jax.ShapeDtypeStruct((spans * CAP, TILE, HD), bf16),
                jax.ShapeDtypeStruct((spans, 8, HD), jnp.int32),
            ),
            in_specs=[smem, vmem],
            out_specs=(smem, vmem, vmem),
            scratch_shapes=[pltpu.SMEM((spans * CAP,), jnp.int32), pltpu.SMEM((spans * CAP,), jnp.int32)],
            name="pack_far",
        )(far_offsets.reshape(HEADS * FAR), q)
        out = pl.pallas_call(
            lambda *refs: fused(spans, rows_ha, cols_wa, *refs),
            out_shape=jax.ShapeDtypeStruct((TILE, HEADS * HD), bf16),
            in_specs=[smem, any_space, any_space, any_space, any_space],
            out_specs=vmem,
            scratch_shapes=[
                tiles(9, NC), pltpu.VMEM((HEADS, TT, 2, TILE, HD), bf16), tiles(9, NC), lines(9, NC),
                tiles(6, NC), lines(6, NC), tiles(NC), lines(NC), tiles(NC), lines(NC),
                tiles(NC), lines(NC), tiles(NC), lines(NC),
                pltpu.VMEM((spans * CAP, TILE, HD), bf16), pltpu.VMEM((spans, 8, HD), jnp.int32),
                pltpu.SMEM((8, HD), jnp.int32),
                pltpu.VMEM((spans * CAP, TILE, HD), bf16), lines(spans),
                pltpu.VMEM((spans * CAP, TILE, HD), bf16), lines(spans),
                pltpu.VMEM((spans * CAP, 1, TILE), f32), pltpu.VMEM((2, TILE, HD), f32),
                pltpu.SemaphoreType.DMA((HEADS,)), pltpu.SemaphoreType.DMA((NC,)), pltpu.SemaphoreType.DMA,
                *sems(NC), *sems(NC), *sems(6, NC), *sems(6, NC), *sems(6, NC),
                *sems(NC), *sems(NC), *sems(NC), *sems(NC),
                *sems(spans), *sems(spans), *sems(spans), *sems(spans),
            ],
            compiler_params=pltpu.CompilerParams(has_side_effects=True, vmem_limit_bytes=67043328),
            name="fused",
        )(slots, q, keys_values[0, 0], qf, qt)
        return out[None, None]

    placed = (
        P("ha", "wa", None, None),
        P("ha", "wa", None, None, None, None),
        P("wa", "ha", None, None),
    )
    return jax.shard_map(
        on_device, mesh=mesh, in_specs=placed, out_specs=P("ha", "wa", None, None), check_vma=False
    )
```

```python
import jax
import jax.numpy as jnp
from jax import lax
from jax.experimental import pallas as pl
from jax.experimental.pallas import tpu as pltpu
from jax.sharding import PartitionSpec as P

HEADS = 12
HD = 128
TILE = 384
TT = 3
FAR = 2
CAP = 2
NC = 3
HC = HEADS // NC
CW = HC * HD
TO_LOG2 = 1.4426950408889634 / HD**0.5
MESH = pl.DeviceIdType.MESH


def pack_far(off_ref, q_ref, slot_ref, qf_ref, qt_ref, heads, count):
    spans = qf_ref.shape[0] // CAP

    def clear(i, carry):
        heads[i] = 0
        count[i] = 0
        return carry

    lax.fori_loop(0, spans * CAP, clear, 0)
    qf_ref[...] = jnp.zeros_like(qf_ref)

    def place(i, carry):
        offset = off_ref[i]
        taken = count[offset]
        count[offset] = taken + 1
        slot = offset * CAP + jnp.minimum(taken, CAP - 1)
        head = i // FAR
        slot_ref[i] = slot
        heads[slot] = head
        qf_ref[slot] = q_ref[:, pl.ds(pl.multiple_of(head * HD, HD), HD)]
        return carry

    lax.fori_loop(0, HEADS * FAR, place, 0)
    lane = lax.broadcasted_iota(jnp.int32, (8, HD), 1)
    for s in range(spans):
        qt_ref[s] = jnp.where(lane == 0, heads[s * CAP], heads[s * CAP + 1])


def attend(q, k, v_one):
    s = lax.dot_general(q, k, (((1,), (1,)), ((), ())), preferred_element_type=jnp.float32)
    peak = jnp.max(s, axis=1, keepdims=True)
    p = jnp.exp2(s * TO_LOG2 - peak * TO_LOG2)
    both = jnp.dot(p.astype(jnp.bfloat16), v_one, preferred_element_type=jnp.float32)
    total = both[:, HD:]
    return (both[:, :HD] * (1.0 / total)).astype(jnp.bfloat16), peak * TO_LOG2 + jnp.log2(total)


def with_ones(v):
    return jnp.concatenate([v, jnp.ones(v.shape, v.dtype)], axis=1)


def blend_weights(rows):
    peak = rows[0]
    for row in rows[1:]:
        peak = jnp.maximum(peak, row)
    parts = [jnp.exp2(row - peak) for row in rows]
    total = parts[0]
    for part in parts[1:]:
        total = total + part
    inverse = 1.0 / total
    stack = [part * inverse for part in parts]
    stack.append(jnp.zeros((HD - 8 * len(rows), TILE), jnp.float32))
    return jnp.transpose(jnp.concatenate(stack, axis=0)), peak + jnp.log2(total)


def fused(
    spans, rows_ha, cols_wa, slot_ref, q_ref, kv_ref, qf_ref, qt_ref, out_ref,
    QW, KV, O, LO, OI, LI, ZS, ZL, ZI, ZLI, XS, XL, XI, XLI, FQ, TI, TS, FO, FL, FI, FLI, FLX, AC,
    kv_sem, q_sem, t_sem, v_s, v_r, z_s, z_r, h_s, h_r, o_s, o_r, l_s, l_r,
    zo_s, zo_r, zl_s, zl_r, xo_s, xo_r, xl_s, xl_r, fq_s, fq_r, ft_s, ft_r, fo_s, fo_r, fl_s, fl_r,
):
    h = lax.axis_index("ha")
    w = lax.axis_index("wa")
    sign = 1 - 2 * (h % 2)
    partner = h + sign
    z_to = (h + 2 * sign + rows_ha) % rows_ha
    z_from = (h - 2 * sign + rows_ha) % rows_ha
    left = (w + cols_wa - 1) % cols_wa
    right = (w + 1) % cols_wa
    has_left = w > 0
    has_right = w < cols_wa - 1
    has_far_row = (h + 2 * sign >= 0) & (h + 2 * sign < rows_ha)

    def cols_of(c):
        return pl.ds(pl.multiple_of(c * CW, CW), CW)

    def remote(src, dst, ss, rs, ha=None, wa=None):
        return pltpu.make_async_remote_copy(
            src_ref=src, dst_ref=dst, send_sem=ss, recv_sem=rs,
            device_id={"ha": h if ha is None else ha, "wa": w if wa is None else wa},
            device_id_type=MESH,
        )

    def kv_in(c):
        cols = pl.ds(pl.multiple_of(c * HD, HD), HD)
        return pltpu.make_async_copy(kv_ref.at[:, :, :, cols], KV.at[c], kv_sem.at[c])

    def q_in(c):
        return pltpu.make_async_copy(q_ref.at[:, cols_of(c)], QW.at[0, c], q_sem.at[c])

    def send_v(c):
        return remote(q_ref.at[:, cols_of(c)], QW.at[3, c], v_s.at[c], v_r.at[c], ha=partner)

    def send_z(c):
        return remote(QW.at[3, c], QW.at[6, c], z_s.at[c], z_r.at[c], ha=z_to)

    def send_h(r, side, c):
        src = q_ref.at[:, cols_of(c)] if r == 0 else QW.at[3 * r, c]
        i = r * 2 + side
        return remote(
            src, QW.at[3 * r + 2 - side, c], h_s.at[i, c], h_r.at[i, c],
            wa=right if side else left,
        )

    def send_o(r, side, c):
        i = r * 2 + side
        return (
            remote(O.at[3 * r + 1 + side, c], OI.at[r * 2 + 1 - side, c], o_s.at[i, c], o_r.at[i, c],
                   wa=right if side else left),
            remote(LO.at[3 * r + 1 + side, c], LI.at[r * 2 + 1 - side, c], l_s.at[i, c], l_r.at[i, c],
                   wa=right if side else left),
        )

    def send_zo(c):
        return (
            remote(ZS.at[c], ZI.at[c], zo_s.at[c], zo_r.at[c], ha=z_from),
            remote(ZL.at[c], ZLI.at[c], zl_s.at[c], zl_r.at[c], ha=z_from),
        )

    def send_xo(c):
        return (
            remote(XS.at[c], XI.at[c], xo_s.at[c], xo_r.at[c], ha=partner),
            remote(XL.at[c], XLI.at[c], xl_s.at[c], xl_r.at[c], ha=partner),
        )

    def send_fq(s):
        owner = (w + 1 + s) % cols_wa
        return (
            remote(qt_ref.at[s], TI.at[s], ft_s.at[s], ft_r.at[s], wa=owner),
            remote(qf_ref.at[pl.ds(s * CAP, CAP)], FQ.at[pl.ds(s * CAP, CAP)], fq_s.at[s], fq_r.at[s], wa=owner),
        )

    def send_fo(s):
        asker = (w + 2 * cols_wa - 1 - s) % cols_wa
        return (
            remote(FO.at[pl.ds(s * CAP, CAP)], FI.at[pl.ds(s * CAP, CAP)], fo_s.at[s], fo_r.at[s], wa=asker),
            remote(FL.at[s], FLI.at[s], fl_s.at[s], fl_r.at[s], wa=asker),
        )

    def chunks(step):
        def run(c, carry):
            step(c)
            return carry

        lax.fori_loop(0, NC, run, 0)

    def kv_start(head, carry):
        kv_in(head).start()
        return carry

    lax.fori_loop(0, HEADS, kv_start, 0)

    @chunks
    def _(c):
        q_in(c).start()
        send_v(c).start()

    @chunks
    def _(c):
        send_h(0, 0, c).start()
        send_h(0, 1, c).start()

    def far_out(k, carry):
        for copy in send_fq(k * 4 % spans):
            copy.start()
        return carry

    lax.fori_loop(0, spans, far_out, 0)

    AC[...] = jnp.zeros_like(AC)
    lane = lax.broadcasted_iota(jnp.int32, (TILE, HD), 1)

    def head_cols(hh):
        return pl.ds(pl.multiple_of(hh * HD, HD), HD)

    def keys_values_of(head):
        k = KV[head, :, 0].reshape(TT * TILE, HD)
        v = KV[head, :, 1].reshape(TT * TILE, HD)
        return k, with_ones(v)

    def pair(a, b, c):
        def step(hh, carry):
            cols = head_cols(hh)
            k, v = keys_values_of(c * HC + hh)
            for i, slot in enumerate((a, b)):
                o, l = attend(QW[slot, c, :, cols], k, v)
                O[slot, c, :, cols] = o
                AC[i] = jnp.where(lane == hh, l, AC[i])
            return carry

        lax.fori_loop(0, HC, step, 0)
        for i, slot in enumerate((a, b)):
            LO[slot, c] = jnp.transpose(AC[i])[:8]

    @chunks
    def _(c):
        for hh in range(HC):
            kv_in(c * HC + hh).wait()
        q_in(c).wait()

        def step(half, carry):
            for e in range(2):
                hh = half * 2 + e
                cols = head_cols(hh)
                k, v = keys_values_of(c * HC + hh)
                o, l = attend(QW[0, c, :, cols], k, v)
                O[0, c, :, cols] = o
                AC[0] = jnp.where(lane == hh, l, AC[0])
            return carry

        lax.fori_loop(0, HC // 2, step, 0)
        LO[0, c] = jnp.transpose(AC[0])[:8]

    def give_back(r, c):
        for side in range(2):
            for copy in send_o(r, side, c):
                copy.start()

    @chunks
    def _(c):
        send_h(0, 0, c).wait_recv()
        send_h(0, 1, c).wait_recv()
        pair(1, 2, c)
        give_back(0, c)
        send_v(c).wait_recv()
        send_z(c).start()
        send_h(1, 0, c).start()
        send_h(1, 1, c).start()

    @chunks
    def _(c):
        send_z(c).wait_recv()
        send_h(2, 0, c).start()
        send_h(2, 1, c).start()
        pair(3, 6, c)

    def far_step(k, carry):
        s = k * 4 % spans
        for copy in send_fq(s):
            copy.wait_recv()
        table = pltpu.make_async_copy(TI.at[s], TS, t_sem)
        table.start()
        table.wait()
        for p in range(CAP):
            head = TS[0, p]
            o, l = attend(FQ[s * CAP + p], KV[head, 1, 0], with_ones(KV[head, 1, 1]))
            FO[s * CAP + p] = o
            AC[0] = jnp.where(lane == p, l, AC[0])
        FL[s] = jnp.transpose(AC[0])[:8]
        for copy in send_fo(s):
            copy.start()
        return carry

    lax.fori_loop(0, spans, far_step, 0)

    for r in (2, 1):

        @chunks
        def _(c):
            send_h(r, 0, c).wait_recv()
            send_h(r, 1, c).wait_recv()
            pair(3 * r + 1, 3 * r + 2, c)
            give_back(r, c)

    def arrived(r, c):
        for side in range(2):
            for copy in send_o(r, side, c):
                copy.wait_recv()

    def masked(row, ok):
        return jnp.where(ok, row, -1e30)

    def row_parts(r, c):
        outs = [O.at[3 * r, c], OI.at[2 * r, c], OI.at[2 * r + 1, c]]
        rows = [LO[3 * r, c], masked(LI[2 * r, c], has_left), masked(LI[2 * r + 1, c], has_right)]
        return outs, rows

    def blend(outs, weights, hh):
        total = None
        for i, o in enumerate(outs):
            term = o.astype(jnp.float32) * weights[:, i * 8 + hh : i * 8 + hh + 1]
            total = term if total is None else total + term
        return total.astype(jnp.bfloat16)

    @chunks
    def _(c):
        arrived(2, c)
        outs, rows = row_parts(2, c)
        weights, joint = blend_weights(rows)
        ZL[c] = joint
        for hh in range(HC):
            cols = slice(hh * HD, (hh + 1) * HD)
            ZS[c, :, cols] = blend([o[:, cols] for o in outs], weights, hh)
        for copy in send_zo(c):
            copy.start()

    @chunks
    def _(c):
        arrived(1, c)
        for copy in send_zo(c):
            copy.wait_recv()
        outs, rows = row_parts(1, c)
        outs.append(ZI.at[c])
        rows.append(masked(ZLI[c], has_far_row))
        weights, joint = blend_weights(rows)
        XL[c] = joint
        for hh in range(HC):
            cols = slice(hh * HD, (hh + 1) * HD)
            XS[c, :, cols] = blend([o[:, cols] for o in outs], weights, hh)
        for copy in send_xo(c):
            copy.start()

    def far_in(s, carry):
        for copy in send_fo(s):
            copy.wait_recv()
        for p in range(CAP):
            FLX[s * CAP + p] = FLI[s, p : p + 1, :]
        return carry

    lax.fori_loop(0, spans, far_in, 0)

    @chunks
    def _(c):
        arrived(0, c)
        for copy in send_xo(c):
            copy.wait_recv()
        outs, rows = row_parts(0, c)
        outs.append(XI.at[c])
        rows.append(XLI[c])
        far = [[slot_ref[(c * HC + hh) * FAR + f] for hh in range(HC)] for f in range(FAR)]
        for f in range(FAR):
            lines = [FLX[slot] for slot in far[f]]
            lines.append(jnp.zeros((8 - HC, TILE), jnp.float32))
            rows.append(jnp.concatenate(lines, axis=0))
        weights, _joint = blend_weights(rows)
        for hh in range(HC):
            cols = slice(hh * HD, (hh + 1) * HD)
            values = [o[:, cols] for o in outs] + [FI[far[f][hh]] for f in range(FAR)]
            out_ref[:, pl.ds(pl.multiple_of(c * CW + hh * HD, HD), HD)] = blend(values, weights, hh)

    @chunks
    def _(c):
        send_v(c).wait_send()
        send_z(c).wait_send()
        for r in range(3):
            for side in range(2):
                send_h(r, side, c).wait_send()
                for copy in send_o(r, side, c):
                    copy.wait_send()
        for copy in send_zo(c) + send_xo(c):
            copy.wait_send()

    def far_done(s, carry):
        for copy in send_fq(s) + send_fo(s):
            copy.wait_send()
        return carry

    lax.fori_loop(0, spans, far_done, 0)


def solution(mesh):
    rows_ha, cols_wa = mesh.shape["ha"], mesh.shape["wa"]
    spans = cols_wa - 1
    bf16, f32 = jnp.bfloat16, jnp.float32
    any_space = pl.BlockSpec(memory_space=pl.ANY)
    smem = pl.BlockSpec(memory_space=pltpu.SMEM)
    vmem = pl.BlockSpec(memory_space=pltpu.VMEM)

    def tiles(*lead):
        return pltpu.VMEM((*lead, TILE, CW), bf16)

    def lines(*lead):
        return pltpu.VMEM((*lead, 8, TILE), f32)

    def sems(*dims):
        return [pltpu.SemaphoreType.DMA(dims)] * 2

    def on_device(queries, keys_values, far_offsets):
        q = queries[0, 0]
        slots, qf, qt = pl.pallas_call(
            pack_far,
            out_shape=(
                jax.ShapeDtypeStruct((HEADS * FAR,), jnp.int32),
                jax.ShapeDtypeStruct((spans * CAP, TILE, HD), bf16),
                jax.ShapeDtypeStruct((spans, 8, HD), jnp.int32),
            ),
            in_specs=[smem, vmem],
            out_specs=(smem, vmem, vmem),
            scratch_shapes=[pltpu.SMEM((spans * CAP,), jnp.int32), pltpu.SMEM((spans * CAP,), jnp.int32)],
            name="pack_far",
        )(far_offsets.reshape(HEADS * FAR), q)
        out = pl.pallas_call(
            lambda *refs: fused(spans, rows_ha, cols_wa, *refs),
            out_shape=jax.ShapeDtypeStruct((TILE, HEADS * HD), bf16),
            in_specs=[smem, any_space, any_space, any_space, any_space],
            out_specs=vmem,
            scratch_shapes=[
                tiles(9, NC), pltpu.VMEM((HEADS, TT, 2, TILE, HD), bf16), tiles(9, NC), lines(9, NC),
                tiles(6, NC), lines(6, NC), tiles(NC), lines(NC), tiles(NC), lines(NC),
                tiles(NC), lines(NC), tiles(NC), lines(NC),
                pltpu.VMEM((spans * CAP, TILE, HD), bf16), pltpu.VMEM((spans, 8, HD), jnp.int32),
                pltpu.SMEM((8, HD), jnp.int32),
                pltpu.VMEM((spans * CAP, TILE, HD), bf16), lines(spans),
                pltpu.VMEM((spans * CAP, TILE, HD), bf16), lines(spans),
                pltpu.VMEM((spans * CAP, 1, TILE), f32), pltpu.VMEM((2, TILE, HD), f32),
                pltpu.SemaphoreType.DMA((HEADS,)), pltpu.SemaphoreType.DMA((NC,)), pltpu.SemaphoreType.DMA,
                *sems(NC), *sems(NC), *sems(6, NC), *sems(6, NC), *sems(6, NC),
                *sems(NC), *sems(NC), *sems(NC), *sems(NC),
                *sems(spans), *sems(spans), *sems(spans), *sems(spans),
            ],
            compiler_params=pltpu.CompilerParams(has_side_effects=True, vmem_limit_bytes=67043328),
            name="fused",
        )(slots, q, keys_values[0, 0], qf, qt)
        return out[None, None]

    placed = (
        P("ha", "wa", None, None),
        P("ha", "wa", None, None, None, None),
        P("wa", "ha", None, None),
    )
    return jax.shard_map(
        on_device, mesh=mesh, in_specs=placed, out_specs=P("ha", "wa", None, None), check_vma=False
    )
```

```python
import jax
import jax.numpy as jnp
from jax import lax
from jax.experimental import pallas as pl
from jax.experimental.pallas import tpu as pltpu
from jax.sharding import PartitionSpec as P

HEADS = 12
HD = 128
TILE = 384
TT = 3
FAR = 2
CAP = 2
NC = 3
HC = HEADS // NC
CW = HC * HD
TO_LOG2 = 1.4426950408889634 / HD**0.5
MESH = pl.DeviceIdType.MESH


def pack_far(off_ref, q_ref, slot_ref, qf_ref, qt_ref, heads, count):
    spans = qf_ref.shape[0] // CAP

    def clear(i, carry):
        heads[i] = 0
        count[i] = 0
        return carry

    lax.fori_loop(0, spans * CAP, clear, 0)
    qf_ref[...] = jnp.zeros_like(qf_ref)

    def place(i, carry):
        offset = off_ref[i]
        taken = count[offset]
        count[offset] = taken + 1
        slot = offset * CAP + jnp.minimum(taken, CAP - 1)
        head = i // FAR
        slot_ref[i] = slot
        heads[slot] = head
        qf_ref[slot] = q_ref[:, pl.ds(pl.multiple_of(head * HD, HD), HD)]
        return carry

    lax.fori_loop(0, HEADS * FAR, place, 0)
    lane = lax.broadcasted_iota(jnp.int32, (8, HD), 1)
    for s in range(spans):
        qt_ref[s] = jnp.where(lane == 0, heads[s * CAP], heads[s * CAP + 1])


def attend(q, k, v_one):
    s = lax.dot_general(q, k, (((1,), (1,)), ((), ())), preferred_element_type=jnp.float32)
    peak = jnp.max(s, axis=1, keepdims=True)
    p = jnp.exp2(s * TO_LOG2 - peak * TO_LOG2)
    both = jnp.dot(p.astype(jnp.bfloat16), v_one, preferred_element_type=jnp.float32)
    total = both[:, HD:]
    return (both[:, :HD] * (1.0 / total)).astype(jnp.bfloat16), peak * TO_LOG2 + jnp.log2(total)


def with_ones(v):
    return jnp.concatenate([v, jnp.ones(v.shape, v.dtype)], axis=1)


def blend_weights(rows):
    peak = rows[0]
    for row in rows[1:]:
        peak = jnp.maximum(peak, row)
    parts = [jnp.exp2(row - peak) for row in rows]
    total = parts[0]
    for part in parts[1:]:
        total = total + part
    inverse = 1.0 / total
    stack = [part * inverse for part in parts]
    stack.append(jnp.zeros((HD - 8 * len(rows), TILE), jnp.float32))
    return jnp.transpose(jnp.concatenate(stack, axis=0)), peak + jnp.log2(total)


def fused(
    spans, rows_ha, cols_wa, slot_ref, q_ref, kv_ref, qf_ref, qt_ref, out_ref,
    QW, KV, O, LO, OI, LI, ZS, ZL, ZI, ZLI, XS, XL, XI, XLI, FQ, TI, TS, FO, FL, FI, FLI, FLX, AC,
    kv_sem, q_sem, t_sem, v_s, v_r, z_s, z_r, h_s, h_r, o_s, o_r, l_s, l_r,
    zo_s, zo_r, zl_s, zl_r, xo_s, xo_r, xl_s, xl_r, fq_s, fq_r, ft_s, ft_r, fo_s, fo_r, fl_s, fl_r,
):
    h = lax.axis_index("ha")
    w = lax.axis_index("wa")
    sign = 1 - 2 * (h % 2)
    partner = h + sign
    z_to = (h + 2 * sign + rows_ha) % rows_ha
    z_from = (h - 2 * sign + rows_ha) % rows_ha
    left = (w + cols_wa - 1) % cols_wa
    right = (w + 1) % cols_wa
    has_left = w > 0
    has_right = w < cols_wa - 1
    has_far_row = (h + 2 * sign >= 0) & (h + 2 * sign < rows_ha)

    def cols_of(c):
        return pl.ds(pl.multiple_of(c * CW, CW), CW)

    def remote(src, dst, ss, rs, ha=None, wa=None):
        return pltpu.make_async_remote_copy(
            src_ref=src, dst_ref=dst, send_sem=ss, recv_sem=rs,
            device_id={"ha": h if ha is None else ha, "wa": w if wa is None else wa},
            device_id_type=MESH,
        )

    def kv_in(c):
        cols = pl.ds(pl.multiple_of(c * HD, HD), HD)
        return pltpu.make_async_copy(kv_ref.at[:, :, :, cols], KV.at[c], kv_sem.at[c])

    def q_in(c):
        return pltpu.make_async_copy(q_ref.at[:, cols_of(c)], QW.at[0, c], q_sem.at[c])

    def send_v(c):
        return remote(q_ref.at[:, cols_of(c)], QW.at[3, c], v_s.at[c], v_r.at[c], ha=partner)

    def send_z(c):
        return remote(QW.at[3, c], QW.at[6, c], z_s.at[c], z_r.at[c], ha=z_to)

    def send_h(r, side, c):
        src = q_ref.at[:, cols_of(c)] if r == 0 else QW.at[3 * r, c]
        i = r * 2 + side
        return remote(
            src, QW.at[3 * r + 2 - side, c], h_s.at[i, c], h_r.at[i, c],
            wa=right if side else left,
        )

    def send_o(r, side, c):
        i = r * 2 + side
        return (
            remote(O.at[3 * r + 1 + side, c], OI.at[r * 2 + 1 - side, c], o_s.at[i, c], o_r.at[i, c],
                   wa=right if side else left),
            remote(LO.at[3 * r + 1 + side, c], LI.at[r * 2 + 1 - side, c], l_s.at[i, c], l_r.at[i, c],
                   wa=right if side else left),
        )

    def send_zo(c):
        return (
            remote(ZS.at[c], ZI.at[c], zo_s.at[c], zo_r.at[c], ha=z_from),
            remote(ZL.at[c], ZLI.at[c], zl_s.at[c], zl_r.at[c], ha=z_from),
        )

    def send_xo(c):
        return (
            remote(XS.at[c], XI.at[c], xo_s.at[c], xo_r.at[c], ha=partner),
            remote(XL.at[c], XLI.at[c], xl_s.at[c], xl_r.at[c], ha=partner),
        )

    def send_fq(s):
        owner = (w + 1 + s) % cols_wa
        return (
            remote(qt_ref.at[s], TI.at[s], ft_s.at[s], ft_r.at[s], wa=owner),
            remote(qf_ref.at[pl.ds(s * CAP, CAP)], FQ.at[pl.ds(s * CAP, CAP)], fq_s.at[s], fq_r.at[s], wa=owner),
        )

    def send_fo(s):
        asker = (w + 2 * cols_wa - 1 - s) % cols_wa
        return (
            remote(FO.at[pl.ds(s * CAP, CAP)], FI.at[pl.ds(s * CAP, CAP)], fo_s.at[s], fo_r.at[s], wa=asker),
            remote(FL.at[s], FLI.at[s], fl_s.at[s], fl_r.at[s], wa=asker),
        )

    def chunks(step):
        def run(c, carry):
            step(c)
            return carry

        lax.fori_loop(0, NC, run, 0)

    def kv_start(head, carry):
        kv_in(head).start()
        return carry

    lax.fori_loop(0, HEADS, kv_start, 0)

    @chunks
    def _(c):
        q_in(c).start()
        send_v(c).start()

    @chunks
    def _(c):
        send_h(0, 0, c).start()
        send_h(0, 1, c).start()

    def far_out(k, carry):
        for copy in send_fq(k * 7 % spans):
            copy.start()
        return carry

    lax.fori_loop(0, spans, far_out, 0)

    AC[...] = jnp.zeros_like(AC)
    lane = lax.broadcasted_iota(jnp.int32, (TILE, HD), 1)

    def head_cols(hh):
        return pl.ds(pl.multiple_of(hh * HD, HD), HD)

    def keys_values_of(head):
        k = KV[head, :, 0].reshape(TT * TILE, HD)
        v = KV[head, :, 1].reshape(TT * TILE, HD)
        return k, with_ones(v)

    def pair(a, b, c):
        def step(hh, carry):
            cols = head_cols(hh)
            k, v = keys_values_of(c * HC + hh)
            for i, slot in enumerate((a, b)):
                o, l = attend(QW[slot, c, :, cols], k, v)
                O[slot, c, :, cols] = o
                AC[i] = jnp.where(lane == hh, l, AC[i])
            return carry

        lax.fori_loop(0, HC, step, 0)
        for i, slot in enumerate((a, b)):
            LO[slot, c] = jnp.transpose(AC[i])[:8]

    @chunks
    def _(c):
        for hh in range(HC):
            kv_in(c * HC + hh).wait()
        q_in(c).wait()

        def step(half, carry):
            for e in range(2):
                hh = half * 2 + e
                cols = head_cols(hh)
                k, v = keys_values_of(c * HC + hh)
                o, l = attend(QW[0, c, :, cols], k, v)
                O[0, c, :, cols] = o
                AC[0] = jnp.where(lane == hh, l, AC[0])
            return carry

        lax.fori_loop(0, HC // 2, step, 0)
        LO[0, c] = jnp.transpose(AC[0])[:8]

    def give_back(r, c):
        for side in range(2):
            for copy in send_o(r, side, c):
                copy.start()

    @chunks
    def _(c):
        send_h(0, 0, c).wait_recv()
        send_h(0, 1, c).wait_recv()
        pair(1, 2, c)
        give_back(0, c)
        send_v(c).wait_recv()
        send_z(c).start()
        send_h(1, 0, c).start()
        send_h(1, 1, c).start()

    @chunks
    def _(c):
        send_z(c).wait_recv()
        send_h(2, 0, c).start()
        send_h(2, 1, c).start()
        pair(3, 6, c)

    def far_step(k, carry):
        s = k * 7 % spans
        for copy in send_fq(s):
            copy.wait_recv()
        table = pltpu.make_async_copy(TI.at[s], TS, t_sem)
        table.start()
        table.wait()
        for p in range(CAP):
            head = TS[0, p]
            o, l = attend(FQ[s * CAP + p], KV[head, 1, 0], with_ones(KV[head, 1, 1]))
            FO[s * CAP + p] = o
            AC[0] = jnp.where(lane == p, l, AC[0])
        FL[s] = jnp.transpose(AC[0])[:8]
        for copy in send_fo(s):
            copy.start()
        return carry

    lax.fori_loop(0, spans, far_step, 0)

    for r in (2, 1):

        @chunks
        def _(c):
            send_h(r, 0, c).wait_recv()
            send_h(r, 1, c).wait_recv()
            pair(3 * r + 1, 3 * r + 2, c)
            give_back(r, c)

    def arrived(r, c):
        for side in range(2):
            for copy in send_o(r, side, c):
                copy.wait_recv()

    def masked(row, ok):
        return jnp.where(ok, row, -1e30)

    def row_parts(r, c):
        outs = [O.at[3 * r, c], OI.at[2 * r, c], OI.at[2 * r + 1, c]]
        rows = [LO[3 * r, c], masked(LI[2 * r, c], has_left), masked(LI[2 * r + 1, c], has_right)]
        return outs, rows

    def blend(outs, weights, hh):
        total = None
        for i, o in enumerate(outs):
            term = o.astype(jnp.float32) * weights[:, i * 8 + hh : i * 8 + hh + 1]
            total = term if total is None else total + term
        return total.astype(jnp.bfloat16)

    @chunks
    def _(c):
        arrived(2, c)
        outs, rows = row_parts(2, c)
        weights, joint = blend_weights(rows)
        ZL[c] = joint
        for hh in range(HC):
            cols = slice(hh * HD, (hh + 1) * HD)
            ZS[c, :, cols] = blend([o[:, cols] for o in outs], weights, hh)
        for copy in send_zo(c):
            copy.start()

    @chunks
    def _(c):
        arrived(1, c)
        for copy in send_zo(c):
            copy.wait_recv()
        outs, rows = row_parts(1, c)
        outs.append(ZI.at[c])
        rows.append(masked(ZLI[c], has_far_row))
        weights, joint = blend_weights(rows)
        XL[c] = joint
        for hh in range(HC):
            cols = slice(hh * HD, (hh + 1) * HD)
            XS[c, :, cols] = blend([o[:, cols] for o in outs], weights, hh)
        for copy in send_xo(c):
            copy.start()

    def far_in(s, carry):
        for copy in send_fo(s):
            copy.wait_recv()
        for p in range(CAP):
            FLX[s * CAP + p] = FLI[s, p : p + 1, :]
        return carry

    lax.fori_loop(0, spans, far_in, 0)

    @chunks
    def _(c):
        arrived(0, c)
        for copy in send_xo(c):
            copy.wait_recv()
        outs, rows = row_parts(0, c)
        outs.append(XI.at[c])
        rows.append(XLI[c])
        far = [[slot_ref[(c * HC + hh) * FAR + f] for hh in range(HC)] for f in range(FAR)]
        for f in range(FAR):
            lines = [FLX[slot] for slot in far[f]]
            lines.append(jnp.zeros((8 - HC, TILE), jnp.float32))
            rows.append(jnp.concatenate(lines, axis=0))
        weights, _joint = blend_weights(rows)
        for hh in range(HC):
            cols = slice(hh * HD, (hh + 1) * HD)
            values = [o[:, cols] for o in outs] + [FI[far[f][hh]] for f in range(FAR)]
            out_ref[:, pl.ds(pl.multiple_of(c * CW + hh * HD, HD), HD)] = blend(values, weights, hh)

    @chunks
    def _(c):
        send_v(c).wait_send()
        send_z(c).wait_send()
        for r in range(3):
            for side in range(2):
                send_h(r, side, c).wait_send()
                for copy in send_o(r, side, c):
                    copy.wait_send()
        for copy in send_zo(c) + send_xo(c):
            copy.wait_send()

    def far_done(s, carry):
        for copy in send_fq(s) + send_fo(s):
            copy.wait_send()
        return carry

    lax.fori_loop(0, spans, far_done, 0)


def solution(mesh):
    rows_ha, cols_wa = mesh.shape["ha"], mesh.shape["wa"]
    spans = cols_wa - 1
    bf16, f32 = jnp.bfloat16, jnp.float32
    any_space = pl.BlockSpec(memory_space=pl.ANY)
    smem = pl.BlockSpec(memory_space=pltpu.SMEM)
    vmem = pl.BlockSpec(memory_space=pltpu.VMEM)

    def tiles(*lead):
        return pltpu.VMEM((*lead, TILE, CW), bf16)

    def lines(*lead):
        return pltpu.VMEM((*lead, 8, TILE), f32)

    def sems(*dims):
        return [pltpu.SemaphoreType.DMA(dims)] * 2

    def on_device(queries, keys_values, far_offsets):
        q = queries[0, 0]
        slots, qf, qt = pl.pallas_call(
            pack_far,
            out_shape=(
                jax.ShapeDtypeStruct((HEADS * FAR,), jnp.int32),
                jax.ShapeDtypeStruct((spans * CAP, TILE, HD), bf16),
                jax.ShapeDtypeStruct((spans, 8, HD), jnp.int32),
            ),
            in_specs=[smem, vmem],
            out_specs=(smem, vmem, vmem),
            scratch_shapes=[pltpu.SMEM((spans * CAP,), jnp.int32), pltpu.SMEM((spans * CAP,), jnp.int32)],
            name="pack_far",
        )(far_offsets.reshape(HEADS * FAR), q)
        out = pl.pallas_call(
            lambda *refs: fused(spans, rows_ha, cols_wa, *refs),
            out_shape=jax.ShapeDtypeStruct((TILE, HEADS * HD), bf16),
            in_specs=[smem, any_space, any_space, any_space, any_space],
            out_specs=vmem,
            scratch_shapes=[
                tiles(9, NC), pltpu.VMEM((HEADS, TT, 2, TILE, HD), bf16), tiles(9, NC), lines(9, NC),
                tiles(6, NC), lines(6, NC), tiles(NC), lines(NC), tiles(NC), lines(NC),
                tiles(NC), lines(NC), tiles(NC), lines(NC),
                pltpu.VMEM((spans * CAP, TILE, HD), bf16), pltpu.VMEM((spans, 8, HD), jnp.int32),
                pltpu.SMEM((8, HD), jnp.int32),
                pltpu.VMEM((spans * CAP, TILE, HD), bf16), lines(spans),
                pltpu.VMEM((spans * CAP, TILE, HD), bf16), lines(spans),
                pltpu.VMEM((spans * CAP, 1, TILE), f32), pltpu.VMEM((2, TILE, HD), f32),
                pltpu.SemaphoreType.DMA((HEADS,)), pltpu.SemaphoreType.DMA((NC,)), pltpu.SemaphoreType.DMA,
                *sems(NC), *sems(NC), *sems(6, NC), *sems(6, NC), *sems(6, NC),
                *sems(NC), *sems(NC), *sems(NC), *sems(NC),
                *sems(spans), *sems(spans), *sems(spans), *sems(spans),
            ],
            compiler_params=pltpu.CompilerParams(has_side_effects=True, vmem_limit_bytes=67043328),
            name="fused",
        )(slots, q, keys_values[0, 0], qf, qt)
        return out[None, None]

    placed = (
        P("ha", "wa", None, None),
        P("ha", "wa", None, None, None, None),
        P("wa", "ha", None, None),
    )
    return jax.shard_map(
        on_device, mesh=mesh, in_specs=placed, out_specs=P("ha", "wa", None, None), check_vma=False
    )
```
